32 devices in a mesh: gx: 8 (over z, core), gy: 4 (over y, x).
Axes of the slice: x: 2, y: 2, z: 4, core: 2. Of those that a mesh axis runs over, the one named last changes fastest.
Arguments:
- displacement: float32 [3, 64, 32, 128], P(None, 'gx', 'gy'), may hold values from -6 to 6
- velocity: float32 [3, 64, 32, 128], P(None, 'gx', 'gy'), may hold values from -6 to 6
- region: int32 [64, 32, 128], P('gx', 'gy'), may hold values from 0 to 3
- bond_words: int32 [11, 64, 32, 128], P(None, 'gx', 'gy'), may hold values from 0 to 4095, as said below
- moduli: float32 [3, 4], replicated, may hold values from 0.5 to 2
Outputs:
- new_displacement: float32 [3, 64, 32, 128], P(None, 'gx', 'gy')
- new_velocity: float32 [3, 64, 32, 128], P(None, 'gx', 'gy')
The draws below stay inside these ranges and needn't reach their ends.
Inputs may be any that keep to these rules, and one draw needn't show every extreme that they name: `bond_words`: bonds are the integer offsets (a, b, c) with 0 < a*a + b*b + c*c <= 9, numbered 0 to 121 in increasing lexicographic order. Bond q of a node is bit q % 12 of word q // 12 (bit 0 the lowest); a set bit means the bond is intact. A bond whose far end lies outside the grid is never intact; the six bonds of length one are intact wherever they stay inside the grid; bond q of node p equals bond 121 - q of node p + xi_q.
All inputs are finite; a program needn't handle non-finite values.
Results may differ from the reference program's by a relative error of at most 0.00002.
Values sent between devices are 32-bit elements; how exact they have to be, the bound alone decides.
A program may use at most 64 MiB of HBM per device.

```python
import math
import jax
import jax.numpy as jnp
from jax import lax

HORIZON = 3
REGIONS = 4
STEPS = 1
NX = 64
NY = 32
NZ = 128


bits_per_word = 12


def bond_offsets_drawn():
    listed = []
    for shift_x in range(-HORIZON, HORIZON + 1):
        for shift_y in range(-HORIZON, HORIZON + 1):
            for shift_z in range(-HORIZON, HORIZON + 1):
                radius = shift_x * shift_x + shift_y * shift_y + shift_z * shift_z
                if 0 < radius <= HORIZON * HORIZON:
                    listed.append((shift_x, shift_y, shift_z))
    return listed


def draw_bond_words(key, part):
    offsets = bond_offsets_drawn()
    bond_count = len(offsets)
    word_count = (bond_count + bits_per_word - 1) // bits_per_word
    grid_x = lax.broadcasted_iota(jnp.int32, (NX, NY, NZ), 0)
    grid_y = lax.broadcasted_iota(jnp.int32, (NX, NY, NZ), 1)
    grid_z = lax.broadcasted_iota(jnp.int32, (NX, NY, NZ), 2)
    packed = [jnp.zeros((NX, NY, NZ), jnp.int32) for position in range(word_count)]
    for number, offset in enumerate(offsets):
        shift_x, shift_y, shift_z = offset
        partner = min(number, bond_count - 1 - number)
        sampled = jax.random.randint(jax.random.fold_in(key, 1000 + partner), (NX, NY, NZ), 0, 100) < 86
        if number > partner:
            sampled = jnp.roll(sampled, (-shift_x, -shift_y, -shift_z), axis=(0, 1, 2))
        if shift_x * shift_x + shift_y * shift_y + shift_z * shift_z == 1:
            sampled = jnp.ones_like(sampled)
        inside = (grid_x + shift_x >= 0) & (grid_x + shift_x < NX)
        inside = inside & (grid_y + shift_y >= 0) & (grid_y + shift_y < NY)
        inside = inside & (grid_z + shift_z >= 0) & (grid_z + shift_z < NZ)
        bit_value = (sampled & inside).astype(jnp.int32)
        word_index = number // bits_per_word
        bit_shift = number % bits_per_word
        packed[word_index] = packed[word_index] + jnp.left_shift(bit_value, bit_shift)
    return jnp.stack(packed)


def set_ends(values, own_key, smallest, high):
    spot = [jax.random.randint(jax.random.fold_in(own_key, axis), (), 0, length) for axis, length in enumerate(values.shape)]
    main_axis = values.shape.index(max(values.shape))
    next_to = spot[:main_axis] + [(spot[main_axis] + 1) % values.shape[main_axis]] + spot[main_axis + 1:]
    return values.at[tuple(spot)].set(smallest).at[tuple(next_to)].set(high)


def level_of(key, dims, split, low, largest):
    gain = 1.0
    for dim, blocks in split:
        draws = jax.random.uniform(jax.random.fold_in(jax.random.fold_in(key, 6), dim), (blocks,), jnp.float32, low / len(split), largest / len(split))
        gain = gain * jnp.repeat(jnp.exp(draws), dims[dim] // blocks).reshape((-1,) + (1,) * (len(dims) - 1 - dim))
    return gain


def centred(stream_key, extent, deviation, limit, shards=(), dtype=jnp.bfloat16):
    values = jax.random.normal(stream_key, extent, jnp.float32) * deviation
    if len(shards) > 0:
        values = level_of(stream_key, extent, shards, -0.22, 0.18) * values
    return jnp.clip(values, min=-limit, max=limit).astype(dtype)


def setup_inputs(seed: int = 0) -> dict:
    splits = jax.random.split(jax.random.key(seed), 6)
    return {
        "displacement": centred(splits[0], (3, NX, NY, NZ), 1.0, 6.0, ((1, 8), (2, 4)), jnp.float32),
        "velocity": centred(splits[1], (3, NX, NY, NZ), 1.0, 6.0, ((1, 8), (2, 4)), jnp.float32),
        "region": set_ends(jax.random.randint(splits[2], (NX, NY, NZ), 0, REGIONS), jax.random.fold_in(splits[2], 1), 0, REGIONS - 1).astype(jnp.int32),
        "bond_words": draw_bond_words(jax.random.fold_in(splits[5], 71), 0),
        "moduli": jnp.clip(jnp.exp(jax.random.uniform(splits[4], (3, REGIONS), jnp.float32, math.log(0.5), math.log(2.0))), 0.5, 2.0),
    }


time_step = 0.3
bits_per_word = 12

def bond_offsets():
    listed = []
    for shift_x in range(-HORIZON, HORIZON + 1):
        for shift_y in range(-HORIZON, HORIZON + 1):
            for shift_z in range(-HORIZON, HORIZON + 1):
                radius = shift_x * shift_x + shift_y * shift_y + shift_z * shift_z
                if 0 < radius <= HORIZON * HORIZON:
                    listed.append((shift_x, shift_y, shift_z))
    return listed

def bond_length(offset):
    return math.sqrt(offset[0] * offset[0] + offset[1] * offset[1] + offset[2] * offset[2])

def bond_bit(bond_words, number):
    word_index = number // bits_per_word
    bit_shift = number % bits_per_word
    return jnp.bitwise_and(jnp.right_shift(bond_words[word_index], bit_shift), 1).astype(jnp.float32)

def materials(region, moduli):
    fields = jnp.zeros((3,) + region.shape, jnp.float32)
    for material in range(moduli.shape[1]):
        fields = jnp.where((region == material)[None], moduli[:, material][:, None, None, None], fields)
    return (fields[0], fields[1], fields[2])

def window(padded, offset, block_shape):
    start_x = HORIZON + offset[0]
    start_y = HORIZON + offset[1]
    start_z = HORIZON + offset[2]
    return padded[..., start_x:start_x + block_shape[0], start_y:start_y + block_shape[1], start_z:start_z + block_shape[2]]

def stretch_of(padded, centre, offset):
    length = bond_length(offset)
    neighbour = window(padded, offset, centre.shape[1:])
    along = (neighbour[0] - centre[0]) * (offset[0] / length)
    along = along + (neighbour[1] - centre[1]) * (offset[1] / length)
    return along + (neighbour[2] - centre[2]) * (offset[2] / length)

def reference(displacement, velocity, region, bond_words, moduli):
    offsets = bond_offsets()
    block_shape = region.shape
    bulk_modulus, shear_modulus, density = materials(region, moduli)
    volume = jnp.zeros(block_shape, jnp.float32)
    for number, offset in enumerate(offsets):
        volume = volume + bond_bit(bond_words, number) * bond_length(offset)
    pressure_ratio = (3.0 * bulk_modulus - 5.0 * shear_modulus) / volume
    shear_term = 15.0 * shear_modulus / volume
    inverse_mass = 1.0 / density
    margins = ((HORIZON, HORIZON),) * 3
    shear_padded = jnp.pad(shear_term, margins)
    for iteration in range(STEPS):
        padded = jnp.pad(displacement, ((0, 0),) + margins)
        accumulated = jnp.zeros(block_shape, jnp.float32)
        for number, offset in enumerate(offsets):
            accumulated = accumulated + bond_bit(bond_words, number) * stretch_of(padded, displacement, offset)
        dilatation = 3.0 * accumulated / volume
        pressure_term = dilatation * pressure_ratio
        pressure_padded = jnp.pad(pressure_term, margins)
        force_parts = [jnp.zeros(block_shape, jnp.float32) for position in range(3)]
        for number, offset in enumerate(offsets):
            length = bond_length(offset)
            stretch = stretch_of(padded, displacement, offset)
            coefficient = bond_bit(bond_words, number) * (pressure_term + window(pressure_padded, offset, block_shape) + (shear_term + window(shear_padded, offset, block_shape)) * stretch * (1.0 / length))
            for position in range(3):
                force_parts[position] = force_parts[position] + coefficient * (offset[position] / length)
        force_sum = jnp.stack(force_parts)
        velocity = velocity + time_step * force_sum * inverse_mass
        displacement = displacement + time_step * velocity
    return (displacement, velocity)
```

```python
import math

import jax
import jax.numpy as jnp
from jax import lax
from jax.experimental import pallas as pl
from jax.experimental.pallas import tpu as pltpu
from jax.sharding import PartitionSpec as P

HORIZON = 3
time_step = 0.3
bits_per_word = 12

MESH = pl.DeviceIdType.MESH
ROW_PAD = 8
DIRECTIONS = [(dx, dy) for dx in (-1, 0, 1) for dy in (-1, 0, 1) if (dx, dy) != (0, 0)]


def bond_offsets():
    listed = []
    for shift_x in range(-HORIZON, HORIZON + 1):
        for shift_y in range(-HORIZON, HORIZON + 1):
            for shift_z in range(-HORIZON, HORIZON + 1):
                radius = shift_x * shift_x + shift_y * shift_y + shift_z * shift_z
                if 0 < radius <= HORIZON * HORIZON:
                    listed.append((shift_x, shift_y, shift_z))
    return listed


OFFSETS = bond_offsets()
NUMBER = {offset: number for number, offset in enumerate(OFFSETS)}
PAIRS = sorted({(a, b) for a, b, c in OFFSETS})


def squared(offset):
    return offset[0] * offset[0] + offset[1] * offset[1] + offset[2] * offset[2]


def column(a, b):
    found = [(c, NUMBER[(a, b, c)]) for c in range(-HORIZON, HORIZON + 1) if (a, b, c) in NUMBER]
    return [(c, number, squared((a, b, c))) for c, number in found]


def scaled(x, factor):
    return x if factor == 1 else -x if factor == -1 else x * float(factor)


def plus(total, x, factor=1):
    if factor == 0:
        return total
    if total is None:
        return scaled(x, factor)
    if factor == 1:
        return total + x
    if factor == -1:
        return total - x
    return total + x * float(factor)


def ahead(x, c):
    if c == 0:
        return x
    length = x.shape[-1]
    return pltpu.roll(x, (-c) % length, x.ndim - 1)


def kernel(
    disp_hbm,
    region_hbm,
    words_hbm,
    moduli,
    accel,
    disp,
    shear,
    pressure,
    region,
    words,
    weight,
    term,
    ratio,
    inverse_mass,
    local_sem,
    send_sem,
    recv_sem,
):
    block_x, block_y = region.shape[0], region.shape[1]
    gx, gy = lax.axis_index("gx"), lax.axis_index("gy")
    size_x, size_y = lax.axis_size("gx"), lax.axis_size("gy")
    inner_x, inner_y = pl.ds(HORIZON, block_x), pl.ds(ROW_PAD, block_y)

    fetch_disp = pltpu.make_async_copy(disp_hbm, disp.at[:, inner_x, inner_y, :], local_sem.at[0])
    fetch_words = pltpu.make_async_copy(words_hbm, words, local_sem.at[1])
    fetch_region = pltpu.make_async_copy(region_hbm, region, local_sem.at[2])
    fetch_disp.start()
    fetch_words.start()
    fetch_region.start()

    def exists(dx, dy):
        fine = []
        if dx != 0:
            fine.append(gx > 0 if dx < 0 else gx < size_x - 1)
        if dy != 0:
            fine.append(gy > 0 if dy < 0 else gy < size_y - 1)
        return fine[0] if len(fine) == 1 else jnp.logical_and(fine[0], fine[1])

    barrier = pltpu.get_barrier_semaphore()
    for dx, dy in DIRECTIONS:

        @pl.when(exists(dx, dy))
        def _():
            pl.semaphore_signal(
                barrier,
                inc=1,
                device_id={"gx": gx + dx, "gy": gy + dy},
                device_id_type=MESH,
            )

    def clear(ref, lead):
        full_y = pl.ds(ROW_PAD - HORIZON, block_y + 2 * HORIZON)
        for side in (-1, 1):
            first_x = 0 if side < 0 else HORIZON + block_x
            first_y = ROW_PAD - HORIZON if side < 0 else ROW_PAD + block_y

            @pl.when(jnp.logical_not(exists(side, 0)))
            def _():
                where = lead + (pl.ds(first_x, HORIZON), full_y)
                ref[where] = jnp.zeros(ref.at[where].shape, jnp.float32)

            @pl.when(jnp.logical_not(exists(0, side)))
            def _():
                where = lead + (slice(None), pl.ds(first_y, HORIZON))
                ref[where] = jnp.zeros(ref.at[where].shape, jnp.float32)

    clear(disp, (slice(None),))
    clear(shear, ())
    clear(pressure, ())

    neighbours = (
        1 + (gx > 0).astype(jnp.int32) + (gx < size_x - 1).astype(jnp.int32)
    ) * (1 + (gy > 0).astype(jnp.int32) + (gy < size_y - 1).astype(jnp.int32)) - 1
    pl.semaphore_wait(barrier, neighbours)

    def copy_of(ref, lead, turn, place):
        dx, dy = DIRECTIONS[place]
        width = HORIZON if dx == 0 or dy == 0 else HORIZON - 1

        def span(step, base, length):
            if step == 0:
                return pl.ds(base, length), pl.ds(base, length)
            if step > 0:
                return pl.ds(base + length - width, width), pl.ds(base - width, width)
            return pl.ds(base, width), pl.ds(base + length, width)

        from_x, to_x = span(dx, HORIZON, block_x)
        from_y, to_y = span(dy, ROW_PAD, block_y)
        return pltpu.make_async_remote_copy(
            src_ref=ref.at[lead + (from_x, from_y)],
            dst_ref=ref.at[lead + (to_x, to_y)],
            send_sem=send_sem.at[turn, place],
            recv_sem=recv_sem.at[turn, place],
            device_id={"gx": gx + dx, "gy": gy + dy},
            device_id_type=MESH,
        )

    def send(ref, lead, turn):
        for place, (dx, dy) in enumerate(DIRECTIONS):

            @pl.when(exists(dx, dy))
            def _():
                copy_of(ref, lead, turn, place).start()

    def receive(ref, lead, turn):
        for place, (dx, dy) in enumerate(DIRECTIONS):

            @pl.when(exists(-dx, -dy))
            def _():
                copy_of(ref, lead, turn, place).wait_recv()

    def sent(ref, lead, turn):
        for place, (dx, dy) in enumerate(DIRECTIONS):

            @pl.when(exists(dx, dy))
            def _():
                copy_of(ref, lead, turn, place).wait_send()

    fetch_disp.wait()
    send(disp, (slice(None),), 0)

    fetch_words.wait()
    fetch_region.wait()

    def weigh(i, carry):
        by_length = {}
        for number, offset in enumerate(OFFSETS):
            bit = 1 << (number % bits_per_word)
            radius = squared(offset)
            intact = (words[number // bits_per_word, i] & bit) != 0
            value = jnp.where(intact, jnp.float32(1.0 / math.sqrt(radius)), jnp.float32(0.0))
            weight[number, i] = value
            by_length[radius] = plus(by_length.get(radius), value)
        volume = None
        for radius, total in by_length.items():
            volume = plus(volume, total, radius)
        here = region[i]
        fields = []
        for row in range(3):
            field = jnp.zeros(here.shape, jnp.float32)
            for material in range(moduli.shape[1]):
                field = jnp.where(here == material, moduli[row, material], field)
            fields.append(field)
        bulk_modulus, shear_modulus, density = fields
        inverse_volume = 1.0 / volume
        shear[i + HORIZON, inner_y] = 15.0 * shear_modulus * inverse_volume
        pressure_ratio = (3.0 * bulk_modulus - 5.0 * shear_modulus) * inverse_volume
        ratio[i] = 3.0 * pressure_ratio * inverse_volume
        inverse_mass[i] = 1.0 / density
        return carry

    lax.fori_loop(0, block_x, weigh, 0)
    send(shear, (), 1)

    receive(disp, (slice(None),), 0)

    def stretch(i, carry):
        centre = [disp[k, i + HORIZON, inner_y] for k in range(3)]
        total = None
        for a, b in PAIRS:
            rows = pl.ds(ROW_PAD + b, block_y)
            near = [disp[k, i + HORIZON + a, rows] for k in range(3)]
            flat_near, flat_here = None, None
            for k, factor in ((0, a), (1, b)):
                flat_near = plus(flat_near, near[k], factor)
                flat_here = plus(flat_here, centre[k], factor)
            for c, number, radius in column(a, b):
                along = ahead(plus(flat_near, near[2], c), c) - plus(flat_here, centre[2], c)
                part = weight[number, i] * along
                total = plus(total, part)
                term[number, i] = part if radius == 1 else part * (1.0 / radius)
        pressure[i + HORIZON, inner_y] = total * ratio[i]
        return carry

    lax.fori_loop(0, block_x, stretch, 0)
    send(pressure, (), 2)
    receive(shear, (), 1)

    def pull(i, carry):
        shear_here = shear[i + HORIZON, inner_y]
        pressure_here = pressure[i + HORIZON, inner_y]
        force = [None, None, None]
        for a, b in PAIRS:
            near = shear[i + HORIZON + a, pl.ds(ROW_PAD + b, block_y)]
            level = None
            for c, number, radius in column(a, b):
                part = weight[number, i] * pressure_here
                part = part + term[number, i] * (ahead(near, c) + shear_here)
                level = plus(level, part)
                force[2] = plus(force[2], part, c)
            force[0] = plus(force[0], level, a)
            force[1] = plus(force[1], level, b)
        for k in range(3):
            accel[k, i] = force[k]
        return carry

    lax.fori_loop(0, block_x, pull, 0)
    receive(pressure, (), 2)

    def push(i, carry):
        force = [accel[k, i] for k in range(3)]
        for a, b in PAIRS:
            near = pressure[i + HORIZON + a, pl.ds(ROW_PAD + b, block_y)]
            level = None
            for c, number, radius in column(a, b):
                part = weight[number, i] * ahead(near, c)
                level = plus(level, part)
                force[2] = plus(force[2], part, c)
            force[0] = plus(force[0], level, a)
            force[1] = plus(force[1], level, b)
        for k in range(3):
            accel[k, i] = force[k] * inverse_mass[i]
        return carry

    lax.fori_loop(0, block_x, push, 0)
    sent(disp, (slice(None),), 0)
    sent(shear, (), 1)
    sent(pressure, (), 2)


def on_device(displacement, velocity, region, bond_words, moduli):
    block = region.shape
    padded = (block[0] + 2 * HORIZON, block[1] + 2 * ROW_PAD, block[2])
    anywhere = pl.BlockSpec(memory_space=pl.ANY)
    bonds = len(OFFSETS)
    places = len(DIRECTIONS)
    acceleration = pl.pallas_call(
        kernel,
        out_shape=jax.ShapeDtypeStruct(displacement.shape, jnp.float32),
        in_specs=[anywhere] * 3 + [pl.BlockSpec(memory_space=pltpu.SMEM)],
        out_specs=pl.BlockSpec(memory_space=pltpu.VMEM),
        scratch_shapes=[
            pltpu.VMEM((3,) + padded, jnp.float32),
            pltpu.VMEM(padded, jnp.float32),
            pltpu.VMEM(padded, jnp.float32),
            pltpu.VMEM(block, jnp.int32),
            pltpu.VMEM(bond_words.shape, jnp.int32),
            pltpu.VMEM((bonds,) + block, jnp.float32),
            pltpu.VMEM((bonds,) + block, jnp.float32),
            pltpu.VMEM(block, jnp.float32),
            pltpu.VMEM(block, jnp.float32),
            pltpu.SemaphoreType.DMA((3,)),
            pltpu.SemaphoreType.DMA((3, places)),
            pltpu.SemaphoreType.DMA((3, places)),
        ],
        compiler_params=pltpu.CompilerParams(collective_id=0, has_side_effects=True),
        name="peridynamic",
    )(displacement, region, bond_words, moduli)
    new_velocity = velocity + time_step * acceleration
    return (displacement + time_step * new_velocity, new_velocity)


def solution(mesh):
    placed = (
        P(None, "gx", "gy", None),
        P(None, "gx", "gy", None),
        P("gx", "gy", None),
        P(None, "gx", "gy", None),
        P(),
    )
    return jax.shard_map(
        on_device,
        mesh=mesh,
        in_specs=placed,
        out_specs=(P(None, "gx", "gy", None), P(None, "gx", "gy", None)),
        check_vma=False,
    )
```

```python
import math

import jax
import jax.numpy as jnp
from jax import lax
from jax.experimental import pallas as pl
from jax.experimental.pallas import tpu as pltpu
from jax.sharding import PartitionSpec as P

HORIZON = 3
time_step = 0.3
bits_per_word = 12

MESH = pl.DeviceIdType.MESH
ROW_PAD = 8
DIRECTIONS = [(dx, dy) for dx in (-1, 0, 1) for dy in (-1, 0, 1) if (dx, dy) != (0, 0)]


def bond_offsets():
    listed = []
    for shift_x in range(-HORIZON, HORIZON + 1):
        for shift_y in range(-HORIZON, HORIZON + 1):
            for shift_z in range(-HORIZON, HORIZON + 1):
                radius = shift_x * shift_x + shift_y * shift_y + shift_z * shift_z
                if 0 < radius <= HORIZON * HORIZON:
                    listed.append((shift_x, shift_y, shift_z))
    return listed


OFFSETS = bond_offsets()
NUMBER = {offset: number for number, offset in enumerate(OFFSETS)}
PAIRS = sorted({(a, b) for a, b, c in OFFSETS})
LEVEL = [(a, b) for a, b in PAIRS if b == 0]
SLANTED = [(a, b) for a, b in PAIRS if b != 0]
X_FACES = [place for place, (dx, dy) in enumerate(DIRECTIONS) if dy == 0]
Y_FACES = [place for place, (dx, dy) in enumerate(DIRECTIONS) if dx == 0]
CORNERS = [place for place, (dx, dy) in enumerate(DIRECTIONS) if dx != 0 and dy != 0]


def squared(offset):
    return offset[0] * offset[0] + offset[1] * offset[1] + offset[2] * offset[2]


def column(a, b):
    found = [(c, NUMBER[(a, b, c)]) for c in range(-HORIZON, HORIZON + 1) if (a, b, c) in NUMBER]
    return [(c, number, squared((a, b, c))) for c, number in found]


def scaled(x, factor):
    return x if factor == 1 else -x if factor == -1 else x * float(factor)


def plus(total, x, factor=1):
    if factor == 0:
        return total
    if total is None:
        return scaled(x, factor)
    if factor == 1:
        return total + x
    if factor == -1:
        return total - x
    return total + x * float(factor)


def ahead(x, c):
    if c == 0:
        return x
    length = x.shape[-1]
    return pltpu.roll(x, (-c) % length, x.ndim - 1)


def kernel(
    disp_hbm,
    region_hbm,
    words_hbm,
    moduli_hbm,
    accel,
    disp,
    shear,
    pressure,
    region,
    words,
    weight,
    term,
    ratio,
    inverse_mass,
    partial,
    moduli,
    local_sem,
    send_sem,
    recv_sem,
):
    block_x, block_y = region.shape[0], region.shape[1]
    gx, gy = lax.axis_index("gx"), lax.axis_index("gy")
    size_x, size_y = lax.axis_size("gx"), lax.axis_size("gy")
    inner_x, inner_y = pl.ds(HORIZON, block_x), pl.ds(ROW_PAD, block_y)

    fetch_disp = pltpu.make_async_copy(disp_hbm, disp.at[:, inner_x, inner_y, :], local_sem.at[0])
    fetch_words = pltpu.make_async_copy(words_hbm, words, local_sem.at[1])
    fetch_region = pltpu.make_async_copy(region_hbm, region, local_sem.at[2])
    fetch_moduli = pltpu.make_async_copy(moduli_hbm, moduli, local_sem.at[3])
    fetch_disp.start()
    fetch_words.start()
    fetch_moduli.start()
    fetch_region.start()

    def exists(dx, dy):
        fine = []
        if dx != 0:
            fine.append(gx > 0 if dx < 0 else gx < size_x - 1)
        if dy != 0:
            fine.append(gy > 0 if dy < 0 else gy < size_y - 1)
        return fine[0] if len(fine) == 1 else jnp.logical_and(fine[0], fine[1])

    barrier = pltpu.get_barrier_semaphore()
    for dx, dy in DIRECTIONS:

        @pl.when(exists(dx, dy))
        def _():
            pl.semaphore_signal(
                barrier,
                inc=1,
                device_id={"gx": gx + dx, "gy": gy + dy},
                device_id_type=MESH,
            )

    def clear(ref, lead):
        full_y = pl.ds(ROW_PAD - HORIZON, block_y + 2 * HORIZON)
        for side in (-1, 1):
            first_x = 0 if side < 0 else HORIZON + block_x
            first_y = ROW_PAD - HORIZON if side < 0 else ROW_PAD + block_y

            @pl.when(jnp.logical_not(exists(side, 0)))
            def _():
                where = lead + (pl.ds(first_x, HORIZON), full_y)
                ref[where] = jnp.zeros(ref.at[where].shape, jnp.float32)

            @pl.when(jnp.logical_not(exists(0, side)))
            def _():
                where = lead + (slice(None), pl.ds(first_y, HORIZON))
                ref[where] = jnp.zeros(ref.at[where].shape, jnp.float32)

    clear(disp, (slice(None),))
    clear(shear, ())
    clear(pressure, ())

    def copy_of(ref, lead, turn, place):
        dx, dy = DIRECTIONS[place]
        width = HORIZON if dx == 0 or dy == 0 else HORIZON - 1

        def span(step, base, length):
            if step == 0:
                return pl.ds(base, length), pl.ds(base, length)
            if step > 0:
                return pl.ds(base + length - width, width), pl.ds(base - width, width)
            return pl.ds(base, width), pl.ds(base + length, width)

        from_x, to_x = span(dx, HORIZON, block_x)
        from_y, to_y = span(dy, ROW_PAD, block_y)
        return pltpu.make_async_remote_copy(
            src_ref=ref.at[lead + (from_x, from_y)],
            dst_ref=ref.at[lead + (to_x, to_y)],
            send_sem=send_sem.at[turn, place],
            recv_sem=recv_sem.at[turn, place],
            device_id={"gx": gx + dx, "gy": gy + dy},
            device_id_type=MESH,
        )

    def send(ref, lead, turn):
        for place, (dx, dy) in enumerate(DIRECTIONS):

            @pl.when(exists(dx, dy))
            def _():
                copy_of(ref, lead, turn, place).start()

    def receive(ref, lead, turn, places):
        for place in places:
            dx, dy = DIRECTIONS[place]

            @pl.when(exists(-dx, -dy))
            def _():
                copy_of(ref, lead, turn, place).wait_recv()

    def sent(ref, lead, turn):
        for place, (dx, dy) in enumerate(DIRECTIONS):

            @pl.when(exists(dx, dy))
            def _():
                copy_of(ref, lead, turn, place).wait_send()

    fetch_words.wait()
    fetch_region.wait()
    fetch_moduli.wait()

    def planes(body, first, count, step=2):
        def both(j, carry):
            body(first + step * j)
            body(first + step * j + 1)
            return carry

        lax.fori_loop(0, count, both, 0)

    def every(body):
        planes(body, 0, block_x // 2)

    def inner(body):
        planes(body, 2, block_x // 2 - 2)

    def outer(body):
        planes(body, 0, 2, block_x - 2)

    def weigh(i):
        by_length = {}
        for number, offset in enumerate(OFFSETS):
            bit = 1 << (number % bits_per_word)
            radius = squared(offset)
            intact = (words[number // bits_per_word, i] & bit) != 0
            value = jnp.where(intact, jnp.float32(1.0 / math.sqrt(radius)), jnp.float32(0.0))
            weight[number, i] = value
            by_length[radius] = plus(by_length.get(radius), value)
        volume = None
        for radius, total in by_length.items():
            volume = plus(volume, total, radius)
        here = region[i]
        fields = []
        for row in range(3):
            field = jnp.zeros(here.shape, jnp.float32)
            for material in range(moduli.shape[1]):
                field = jnp.where(here == material, moduli[row, material], field)
            fields.append(field)
        bulk_modulus, shear_modulus, density = fields
        inverse_volume = 1.0 / volume
        shear[i + HORIZON, inner_y] = 15.0 * shear_modulus * inverse_volume
        pressure_ratio = (3.0 * bulk_modulus - 5.0 * shear_modulus) * inverse_volume
        ratio[i] = 3.0 * pressure_ratio * inverse_volume
        inverse_mass[i] = 1.0 / density

    every(weigh)
    fetch_disp.wait()
    neighbours = (
        1 + (gx > 0).astype(jnp.int32) + (gx < size_x - 1).astype(jnp.int32)
    ) * (1 + (gy > 0).astype(jnp.int32) + (gy < size_y - 1).astype(jnp.int32)) - 1
    pl.semaphore_wait(barrier, neighbours)

    send(disp, (slice(None),), 0)
    send(shear, (), 1)

    def stretch(i, pairs, total):
        centre = [disp[k, i + HORIZON, inner_y] for k in range(3)]
        for a, b in pairs:
            rows = pl.ds(ROW_PAD + b, block_y)
            near = [disp[k, i + HORIZON + a, rows] for k in range(3)]
            flat_near, flat_here = None, None
            for k, factor in ((0, a), (1, b)):
                flat_near = plus(flat_near, near[k], factor)
                flat_here = plus(flat_here, centre[k], factor)
            for c, number, radius in column(a, b):
                along = ahead(plus(flat_near, near[2], c), c) - plus(flat_here, centre[2], c)
                part = weight[number, i] * along
                total = plus(total, part)
                term[number, i] = part if radius == 1 else part * (1.0 / radius)
        return total

    def stretch_level(i):
        partial[i] = stretch(i, LEVEL, None)

    def stretch_rest(i):
        pressure[i + HORIZON, inner_y] = stretch(i, SLANTED, partial[i]) * ratio[i]

    receive(disp, (slice(None),), 0, X_FACES)
    every(stretch_level)
    receive(disp, (slice(None),), 0, Y_FACES)
    inner(stretch_rest)
    receive(disp, (slice(None),), 0, CORNERS)
    outer(stretch_rest)
    send(pressure, (), 2)
    receive(shear, (), 1, X_FACES + Y_FACES + CORNERS)

    def pull(i):
        shear_here = shear[i + HORIZON, inner_y]
        pressure_here = pressure[i + HORIZON, inner_y]
        force = [None, None, None]
        for a, b in PAIRS:
            near = shear[i + HORIZON + a, pl.ds(ROW_PAD + b, block_y)]
            level = None
            for c, number, radius in column(a, b):
                part = weight[number, i] * pressure_here
                part = part + term[number, i] * (ahead(near, c) + shear_here)
                level = plus(level, part)
                force[2] = plus(force[2], part, c)
            force[0] = plus(force[0], level, a)
            force[1] = plus(force[1], level, b)
        for k in range(3):
            accel[k, i] = force[k]

    def push(i, pairs, mass):
        force = [accel[k, i] for k in range(3)]
        for a, b in pairs:
            near = pressure[i + HORIZON + a, pl.ds(ROW_PAD + b, block_y)]
            level = None
            for c, number, radius in column(a, b):
                part = weight[number, i] * ahead(near, c)
                level = plus(level, part)
                force[2] = plus(force[2], part, c)
            force[0] = plus(force[0], level, a)
            force[1] = plus(force[1], level, b)
        for k in range(3):
            accel[k, i] = force[k] * inverse_mass[i] if mass else force[k]

    every(pull)
    receive(pressure, (), 2, X_FACES)
    every(lambda i: push(i, LEVEL, False))
    receive(pressure, (), 2, Y_FACES)
    inner(lambda i: push(i, SLANTED, True))
    receive(pressure, (), 2, CORNERS)
    outer(lambda i: push(i, SLANTED, True))
    sent(disp, (slice(None),), 0)
    sent(shear, (), 1)
    sent(pressure, (), 2)


def on_device(displacement, velocity, region, bond_words, moduli):
    block = region.shape
    padded = (block[0] + 2 * HORIZON, block[1] + 2 * ROW_PAD, block[2])
    anywhere = pl.BlockSpec(memory_space=pl.ANY)
    bonds = len(OFFSETS)
    places = len(DIRECTIONS)
    acceleration = pl.pallas_call(
        kernel,
        out_shape=pltpu.VMEM(displacement.shape, jnp.float32),
        in_specs=[anywhere] * 4,
        out_specs=pl.BlockSpec(memory_space=pltpu.VMEM),
        scratch_shapes=[
            pltpu.VMEM((3,) + padded, jnp.float32),
            pltpu.VMEM(padded, jnp.float32),
            pltpu.VMEM(padded, jnp.float32),
            pltpu.VMEM(block, jnp.int32),
            pltpu.VMEM(bond_words.shape, jnp.int32),
            pltpu.VMEM((bonds,) + block, jnp.float32),
            pltpu.VMEM((bonds,) + block, jnp.float32),
            pltpu.VMEM(block, jnp.float32),
            pltpu.VMEM(block, jnp.float32),
            pltpu.VMEM(block, jnp.float32),
            pltpu.SMEM(moduli.shape, jnp.float32),
            pltpu.SemaphoreType.DMA((4,)),
            pltpu.SemaphoreType.DMA((3, places)),
            pltpu.SemaphoreType.DMA((3, places)),
        ],
        compiler_params=pltpu.CompilerParams(collective_id=0, has_side_effects=True),
        name="peridynamic",
    )(displacement, region, bond_words, moduli)
    new_velocity = velocity + time_step * acceleration
    return (displacement + time_step * new_velocity, new_velocity)


def solution(mesh):
    placed = (
        P(None, "gx", "gy", None),
        P(None, "gx", "gy", None),
        P("gx", "gy", None),
        P(None, "gx", "gy", None),
        P(),
    )
    return jax.shard_map(
        on_device,
        mesh=mesh,
        in_specs=placed,
        out_specs=(P(None, "gx", "gy", None), P(None, "gx", "gy", None)),
        check_vma=False,
    )
```

```python
import math

import jax
import jax.numpy as jnp
from jax import lax
from jax.experimental import pallas as pl
from jax.experimental.pallas import tpu as pltpu
from jax.sharding import PartitionSpec as P

HORIZON = 3
time_step = 0.3
bits_per_word = 12

MESH = pl.DeviceIdType.MESH
ROW_PAD = 8
DIRECTIONS = [(dx, dy) for dx in (-1, 0, 1) for dy in (-1, 0, 1) if (dx, dy) != (0, 0)]


def bond_offsets():
    listed = []
    for shift_x in range(-HORIZON, HORIZON + 1):
        for shift_y in range(-HORIZON, HORIZON + 1):
            for shift_z in range(-HORIZON, HORIZON + 1):
                radius = shift_x * shift_x + shift_y * shift_y + shift_z * shift_z
                if 0 < radius <= HORIZON * HORIZON:
                    listed.append((shift_x, shift_y, shift_z))
    return listed


OFFSETS = bond_offsets()
NUMBER = {offset: number for number, offset in enumerate(OFFSETS)}
PAIRS = sorted({(a, b) for a, b, c in OFFSETS})
LEVEL = [(a, b) for a, b in PAIRS if b == 0]
SLANTED = [(a, b) for a, b in PAIRS if b != 0]
X_FACES = [place for place, (dx, dy) in enumerate(DIRECTIONS) if dy == 0]
Y_FACES = [place for place, (dx, dy) in enumerate(DIRECTIONS) if dx == 0]
CORNERS = [place for place, (dx, dy) in enumerate(DIRECTIONS) if dx != 0 and dy != 0]


def squared(offset):
    return offset[0] * offset[0] + offset[1] * offset[1] + offset[2] * offset[2]


def column(a, b):
    found = [(c, NUMBER[(a, b, c)]) for c in range(-HORIZON, HORIZON + 1) if (a, b, c) in NUMBER]
    return [(c, number, squared((a, b, c))) for c, number in found]


def scaled(x, factor):
    return x if factor == 1 else -x if factor == -1 else x * float(factor)


def plus(total, x, factor=1):
    if factor == 0:
        return total
    if total is None:
        return scaled(x, factor)
    if factor == 1:
        return total + x
    if factor == -1:
        return total - x
    return total + x * float(factor)


def ahead(x, c):
    if c == 0:
        return x
    length = x.shape[-1]
    return pltpu.roll(x, (-c) % length, x.ndim - 1)


def kernel(
    disp_hbm,
    region_hbm,
    words_hbm,
    moduli_hbm,
    accel,
    disp,
    shear,
    pressure,
    region,
    words,
    weight,
    term,
    ratio,
    inverse_mass,
    partial,
    turned,
    moduli,
    local_sem,
    send_sem,
    recv_sem,
):
    block_x, block_y = region.shape[0], region.shape[1]
    gx, gy = lax.axis_index("gx"), lax.axis_index("gy")
    size_x, size_y = lax.axis_size("gx"), lax.axis_size("gy")
    inner_x, inner_y = pl.ds(HORIZON, block_x), pl.ds(ROW_PAD, block_y)

    fetch_disp = pltpu.make_async_copy(disp_hbm, disp.at[:, inner_x, inner_y, :], local_sem.at[0])
    fetch_words = pltpu.make_async_copy(words_hbm, words, local_sem.at[1])
    fetch_region = pltpu.make_async_copy(region_hbm, region, local_sem.at[2])
    fetch_moduli = pltpu.make_async_copy(moduli_hbm, moduli, local_sem.at[3])
    fetch_disp.start()
    fetch_words.start()
    fetch_moduli.start()
    fetch_region.start()

    def exists(dx, dy):
        fine = []
        if dx != 0:
            fine.append(gx > 0 if dx < 0 else gx < size_x - 1)
        if dy != 0:
            fine.append(gy > 0 if dy < 0 else gy < size_y - 1)
        return fine[0] if len(fine) == 1 else jnp.logical_and(fine[0], fine[1])

    barrier = pltpu.get_barrier_semaphore()
    for dx, dy in DIRECTIONS:

        @pl.when(exists(dx, dy))
        def _():
            pl.semaphore_signal(
                barrier,
                inc=1,
                device_id={"gx": gx + dx, "gy": gy + dy},
                device_id_type=MESH,
            )

    def clear(ref, lead):
        full_y = pl.ds(ROW_PAD - HORIZON, block_y + 2 * HORIZON)
        for side in (-1, 1):
            first_x = 0 if side < 0 else HORIZON + block_x
            first_y = ROW_PAD - HORIZON if side < 0 else ROW_PAD + block_y

            @pl.when(jnp.logical_not(exists(side, 0)))
            def _():
                where = lead + (pl.ds(first_x, HORIZON), full_y)
                ref[where] = jnp.zeros(ref.at[where].shape, jnp.float32)

            @pl.when(jnp.logical_not(exists(0, side)))
            def _():
                where = lead + (slice(None), pl.ds(first_y, HORIZON))
                ref[where] = jnp.zeros(ref.at[where].shape, jnp.float32)

    clear(disp, (slice(None),))
    clear(shear, ())
    clear(pressure, ())

    def copy_of(ref, lead, turn, place):
        dx, dy = DIRECTIONS[place]
        width = HORIZON if dx == 0 or dy == 0 else HORIZON - 1

        def span(step, base, length):
            if step == 0:
                return pl.ds(base, length), pl.ds(base, length)
            if step > 0:
                return pl.ds(base + length - width, width), pl.ds(base - width, width)
            return pl.ds(base, width), pl.ds(base + length, width)

        from_x, to_x = span(dx, HORIZON, block_x)
        from_y, to_y = span(dy, ROW_PAD, block_y)
        return pltpu.make_async_remote_copy(
            src_ref=ref.at[lead + (from_x, from_y)],
            dst_ref=ref.at[lead + (to_x, to_y)],
            send_sem=send_sem.at[turn, place],
            recv_sem=recv_sem.at[turn, place],
            device_id={"gx": gx + dx, "gy": gy + dy},
            device_id_type=MESH,
        )

    def send(ref, lead, turn):
        for place, (dx, dy) in enumerate(DIRECTIONS):

            @pl.when(exists(dx, dy))
            def _():
                copy_of(ref, lead, turn, place).start()

    def receive(ref, lead, turn, places):
        for place in places:
            dx, dy = DIRECTIONS[place]

            @pl.when(exists(-dx, -dy))
            def _():
                copy_of(ref, lead, turn, place).wait_recv()

    def sent(ref, lead, turn):
        for place, (dx, dy) in enumerate(DIRECTIONS):

            @pl.when(exists(dx, dy))
            def _():
                copy_of(ref, lead, turn, place).wait_send()

    fetch_words.wait()
    fetch_region.wait()
    fetch_moduli.wait()

    def planes(body, first, count, step=2):
        def both(j, carry):
            body(first + step * j)
            body(first + step * j + 1)
            return carry

        lax.fori_loop(0, count, both, 0)

    def every(body):
        planes(body, 0, block_x // 2)

    def inner(body):
        planes(body, 2, block_x // 2 - 2)

    def outer(body):
        planes(body, 0, 2, block_x - 2)

    def weigh(i):
        by_length = {}
        for number, offset in enumerate(OFFSETS):
            bit = 1 << (number % bits_per_word)
            radius = squared(offset)
            intact = (words[number // bits_per_word, i] & bit) != 0
            value = jnp.where(intact, jnp.float32(1.0 / math.sqrt(radius)), jnp.float32(0.0))
            weight[number, i] = value
            by_length[radius] = plus(by_length.get(radius), value)
        volume = None
        for radius, total in by_length.items():
            volume = plus(volume, total, radius)
        here = region[i]
        fields = []
        for row in range(3):
            field = jnp.zeros(here.shape, jnp.float32)
            for material in range(moduli.shape[1]):
                field = jnp.where(here == material, moduli[row, material], field)
            fields.append(field)
        bulk_modulus, shear_modulus, density = fields
        inverse_volume = 1.0 / volume
        shear[i + HORIZON, inner_y] = 15.0 * shear_modulus * inverse_volume
        pressure_ratio = (3.0 * bulk_modulus - 5.0 * shear_modulus) * inverse_volume
        ratio[i] = 3.0 * pressure_ratio * inverse_volume
        inverse_mass[i] = 1.0 / density

    every(weigh)
    fetch_disp.wait()
    neighbours = (
        1 + (gx > 0).astype(jnp.int32) + (gx < size_x - 1).astype(jnp.int32)
    ) * (1 + (gy > 0).astype(jnp.int32) + (gy < size_y - 1).astype(jnp.int32)) - 1
    pl.semaphore_wait(barrier, neighbours)

    send(disp, (slice(None),), 0)
    send(shear, (), 1)

    def stretch(i, pairs, total):
        centre = [disp[k, i + HORIZON, inner_y] for k in range(3)]
        for a, b in pairs:
            rows = pl.ds(ROW_PAD + b, block_y)
            near = [disp[k, i + HORIZON + a, rows] for k in range(3)]
            flat_near, flat_here = None, None
            for k, factor in ((0, a), (1, b)):
                flat_near = plus(flat_near, near[k], factor)
                flat_here = plus(flat_here, centre[k], factor)
            for c, number, radius in column(a, b):
                along = ahead(plus(flat_near, near[2], c), c) - plus(flat_here, centre[2], c)
                part = weight[number, i] * along
                total = plus(total, part)
                term[number, i] = part if radius == 1 else part * (1.0 / radius)
        return total

    def stretch_level(i):
        partial[i] = stretch(i, LEVEL, None)

    def stretch_rest(i):
        pressure[i + HORIZON, inner_y] = stretch(i, SLANTED, partial[i]) * ratio[i]

    def turn(i):
        for a, b in SLANTED:
            for c, number, radius in column(a, b):
                if c != 0:
                    turned[number, i] = ahead(weight[number, i], -c)

    every(turn)
    receive(disp, (slice(None),), 0, X_FACES)
    every(stretch_level)
    receive(disp, (slice(None),), 0, Y_FACES)
    inner(stretch_rest)
    receive(disp, (slice(None),), 0, CORNERS)
    outer(stretch_rest)
    send(pressure, (), 2)
    receive(shear, (), 1, X_FACES + Y_FACES + CORNERS)

    def pull(i):
        shear_here = shear[i + HORIZON, inner_y]
        pressure_here = pressure[i + HORIZON, inner_y]
        force = [None, None, None]
        for a, b in PAIRS:
            near = shear[i + HORIZON + a, pl.ds(ROW_PAD + b, block_y)]
            level = None
            for c, number, radius in column(a, b):
                part = weight[number, i] * pressure_here
                part = part + term[number, i] * (ahead(near, c) + shear_here)
                level = plus(level, part)
                force[2] = plus(force[2], part, c)
            force[0] = plus(force[0], level, a)
            force[1] = plus(force[1], level, b)
        for k in range(3):
            accel[k, i] = force[k]

    def push_level(i):
        force = [accel[k, i] for k in range(3)]
        for a, b in LEVEL:
            near = pressure[i + HORIZON + a, inner_y]
            level = None
            for c, number, radius in column(a, b):
                part = weight[number, i] * ahead(near, c)
                level = plus(level, part)
                force[2] = plus(force[2], part, c)
            force[0] = plus(force[0], level, a)
        for k in range(3):
            accel[k, i] = force[k]

    def push_slanted(i):
        force = [accel[k, i] for k in range(3)]
        for c in range(-HORIZON, HORIZON + 1):
            source = weight if c == 0 else turned
            sums = [None, None, None]
            for a in range(-HORIZON, HORIZON + 1):
                row = None
                for b in range(1, HORIZON + 1):
                    if (a, b, c) in NUMBER:
                        up, down = (
                            source[NUMBER[(a, side, c)], i]
                            * pressure[i + HORIZON + a, pl.ds(ROW_PAD + side, block_y)]
                            for side in (b, -b)
                        )
                        row = plus(row, up + down)
                        sums[1] = plus(sums[1], up - down, b)
                if row is not None:
                    sums[0] = plus(sums[0], row, a)
                    sums[2] = plus(sums[2], row)
            if sums[2] is not None:
                for k, factor in ((0, 1), (1, 1), (2, c)):
                    if factor != 0:
                        force[k] = plus(force[k], ahead(sums[k], c), factor)
        for k in range(3):
            accel[k, i] = force[k] * inverse_mass[i]

    every(pull)
    receive(pressure, (), 2, X_FACES)
    every(push_level)
    receive(pressure, (), 2, Y_FACES)
    inner(push_slanted)
    receive(pressure, (), 2, CORNERS)
    outer(push_slanted)
    sent(disp, (slice(None),), 0)
    sent(shear, (), 1)
    sent(pressure, (), 2)


def on_device(displacement, velocity, region, bond_words, moduli):
    block = region.shape
    padded = (block[0] + 2 * HORIZON, block[1] + 2 * ROW_PAD, block[2])
    anywhere = pl.BlockSpec(memory_space=pl.ANY)
    bonds = len(OFFSETS)
    places = len(DIRECTIONS)
    acceleration = pl.pallas_call(
        kernel,
        out_shape=pltpu.VMEM(displacement.shape, jnp.float32),
        in_specs=[anywhere] * 4,
        out_specs=pl.BlockSpec(memory_space=pltpu.VMEM),
        scratch_shapes=[
            pltpu.VMEM((3,) + padded, jnp.float32),
            pltpu.VMEM(padded, jnp.float32),
            pltpu.VMEM(padded, jnp.float32),
            pltpu.VMEM(block, jnp.int32),
            pltpu.VMEM(bond_words.shape, jnp.int32),
            pltpu.VMEM((bonds,) + block, jnp.float32),
            pltpu.VMEM((bonds,) + block, jnp.float32),
            pltpu.VMEM(block, jnp.float32),
            pltpu.VMEM(block, jnp.float32),
            pltpu.VMEM(block, jnp.float32),
            pltpu.VMEM((bonds,) + block, jnp.float32),
            pltpu.SMEM(moduli.shape, jnp.float32),
            pltpu.SemaphoreType.DMA((4,)),
            pltpu.SemaphoreType.DMA((3, places)),
            pltpu.SemaphoreType.DMA((3, places)),
        ],
        compiler_params=pltpu.CompilerParams(collective_id=0, has_side_effects=True),
        name="peridynamic",
    )(displacement, region, bond_words, moduli)
    new_velocity = velocity + time_step * acceleration
    return (displacement + time_step * new_velocity, new_velocity)


def solution(mesh):
    placed = (
        P(None, "gx", "gy", None),
        P(None, "gx", "gy", None),
        P("gx", "gy", None),
        P(None, "gx", "gy", None),
        P(),
    )
    return jax.shard_map(
        on_device,
        mesh=mesh,
        in_specs=placed,
        out_specs=(P(None, "gx", "gy", None), P(None, "gx", "gy", None)),
        check_vma=False,
    )
```

```python
import math

import jax
import jax.numpy as jnp
from jax import lax
from jax.experimental import pallas as pl
from jax.experimental.pallas import tpu as pltpu
from jax.sharding import PartitionSpec as P

HORIZON = 3
time_step = 0.3
bits_per_word = 12

MESH = pl.DeviceIdType.MESH
ROW_PAD = 8
DIRECTIONS = [(dx, dy) for dx in (-1, 0, 1) for dy in (-1, 0, 1) if (dx, dy) != (0, 0)]


def bond_offsets():
    listed = []
    for shift_x in range(-HORIZON, HORIZON + 1):
        for shift_y in range(-HORIZON, HORIZON + 1):
            for shift_z in range(-HORIZON, HORIZON + 1):
                radius = shift_x * shift_x + shift_y * shift_y + shift_z * shift_z
                if 0 < radius <= HORIZON * HORIZON:
                    listed.append((shift_x, shift_y, shift_z))
    return listed


OFFSETS = bond_offsets()
NUMBER = {offset: number for number, offset in enumerate(OFFSETS)}
PAIRS = sorted({(a, b) for a, b, c in OFFSETS})
LEVEL = [(a, b) for a, b in PAIRS if b == 0]
SLANTED = [(a, b) for a, b in PAIRS if b != 0]
X_FACES = [place for place, (dx, dy) in enumerate(DIRECTIONS) if dy == 0]
Y_FACES = [place for place, (dx, dy) in enumerate(DIRECTIONS) if dx == 0]
CORNERS = [place for place, (dx, dy) in enumerate(DIRECTIONS) if dx != 0 and dy != 0]


def squared(offset):
    return offset[0] * offset[0] + offset[1] * offset[1] + offset[2] * offset[2]


def column(a, b):
    found = [(c, NUMBER[(a, b, c)]) for c in range(-HORIZON, HORIZON + 1) if (a, b, c) in NUMBER]
    return [(c, number, squared((a, b, c))) for c, number in found]


def scaled(x, factor):
    return x if factor == 1 else -x if factor == -1 else x * float(factor)


def plus(total, x, factor=1):
    if factor == 0:
        return total
    if total is None:
        return scaled(x, factor)
    if factor == 1:
        return total + x
    if factor == -1:
        return total - x
    return total + x * float(factor)


def ahead(x, c):
    if c == 0:
        return x
    length = x.shape[-1]
    return pltpu.roll(x, (-c) % length, x.ndim - 1)


def kernel(
    disp_hbm,
    region_hbm,
    words_hbm,
    moduli_hbm,
    accel,
    disp,
    shear,
    pressure,
    region,
    words,
    weight,
    term,
    ratio,
    inverse_mass,
    partial,
    turned,
    moduli,
    local_sem,
    send_sem,
    recv_sem,
):
    block_x, block_y = region.shape[0], region.shape[1]
    gx, gy = lax.axis_index("gx"), lax.axis_index("gy")
    size_x, size_y = lax.axis_size("gx"), lax.axis_size("gy")
    inner_x, inner_y = pl.ds(HORIZON, block_x), pl.ds(ROW_PAD, block_y)

    fetch_disp = pltpu.make_async_copy(disp_hbm, disp.at[:, inner_x, inner_y, :], local_sem.at[0])
    fetch_words = pltpu.make_async_copy(words_hbm, words, local_sem.at[1])
    fetch_region = pltpu.make_async_copy(region_hbm, region, local_sem.at[2])
    fetch_moduli = pltpu.make_async_copy(moduli_hbm, moduli, local_sem.at[3])
    fetch_disp.start()
    fetch_words.start()
    fetch_moduli.start()
    fetch_region.start()

    def exists(dx, dy):
        fine = []
        if dx != 0:
            fine.append(gx > 0 if dx < 0 else gx < size_x - 1)
        if dy != 0:
            fine.append(gy > 0 if dy < 0 else gy < size_y - 1)
        return fine[0] if len(fine) == 1 else jnp.logical_and(fine[0], fine[1])

    barrier = pltpu.get_barrier_semaphore()
    for dx, dy in DIRECTIONS:

        @pl.when(exists(dx, dy))
        def _():
            pl.semaphore_signal(
                barrier,
                inc=1,
                device_id={"gx": gx + dx, "gy": gy + dy},
                device_id_type=MESH,
            )

    def clear(ref, lead):
        full_y = pl.ds(ROW_PAD - HORIZON, block_y + 2 * HORIZON)
        for side in (-1, 1):
            first_x = 0 if side < 0 else HORIZON + block_x
            first_y = ROW_PAD - HORIZON if side < 0 else ROW_PAD + block_y

            @pl.when(jnp.logical_not(exists(side, 0)))
            def _():
                where = lead + (pl.ds(first_x, HORIZON), full_y)
                ref[where] = jnp.zeros(ref.at[where].shape, jnp.float32)

            @pl.when(jnp.logical_not(exists(0, side)))
            def _():
                where = lead + (slice(None), pl.ds(first_y, HORIZON))
                ref[where] = jnp.zeros(ref.at[where].shape, jnp.float32)

    clear(disp, (slice(None),))
    clear(shear, ())
    clear(pressure, ())

    def copy_of(ref, lead, turn, place):
        dx, dy = DIRECTIONS[place]
        width = HORIZON if dx == 0 or dy == 0 else HORIZON - 1

        def span(step, base, length):
            if step == 0:
                return pl.ds(base, length), pl.ds(base, length)
            if step > 0:
                return pl.ds(base + length - width, width), pl.ds(base - width, width)
            return pl.ds(base, width), pl.ds(base + length, width)

        from_x, to_x = span(dx, HORIZON, block_x)
        from_y, to_y = span(dy, ROW_PAD, block_y)
        return pltpu.make_async_remote_copy(
            src_ref=ref.at[lead + (from_x, from_y)],
            dst_ref=ref.at[lead + (to_x, to_y)],
            send_sem=send_sem.at[turn, place],
            recv_sem=recv_sem.at[turn, place],
            device_id={"gx": gx + dx, "gy": gy + dy},
            device_id_type=MESH,
        )

    def send(ref, lead, turn):
        for place, (dx, dy) in enumerate(DIRECTIONS):

            @pl.when(exists(dx, dy))
            def _():
                copy_of(ref, lead, turn, place).start()

    def receive(ref, lead, turn, places):
        for place in places:
            dx, dy = DIRECTIONS[place]

            @pl.when(exists(-dx, -dy))
            def _():
                copy_of(ref, lead, turn, place).wait_recv()

    def sent(ref, lead, turn):
        for place, (dx, dy) in enumerate(DIRECTIONS):

            @pl.when(exists(dx, dy))
            def _():
                copy_of(ref, lead, turn, place).wait_send()

    fetch_words.wait()
    fetch_region.wait()
    fetch_moduli.wait()

    def planes(body, first, count, step=2):
        def both(j, carry):
            body(first + step * j)
            body(first + step * j + 1)
            return carry

        if count == 2:
            both(1, both(0, 0))
        else:
            lax.fori_loop(0, count, both, 0)

    def every(body):
        planes(body, 0, block_x // 2)

    def inner(body):
        planes(body, 2, block_x // 2 - 2)

    def outer(body):
        planes(body, 0, 2, block_x - 2)

    def weigh(i):
        by_length = {}
        for number, offset in enumerate(OFFSETS):
            bit = 1 << (number % bits_per_word)
            radius = squared(offset)
            intact = (words[number // bits_per_word, i] & bit) != 0
            value = jnp.where(intact, jnp.float32(1.0 / math.sqrt(radius)), jnp.float32(0.0))
            weight[number, i] = value
            by_length[radius] = plus(by_length.get(radius), value)
        volume = None
        for radius, total in by_length.items():
            volume = plus(volume, total, radius)
        here = region[i]
        fields = []
        for row in range(3):
            field = jnp.zeros(here.shape, jnp.float32)
            for material in range(moduli.shape[1]):
                field = jnp.where(here == material, moduli[row, material], field)
            fields.append(field)
        bulk_modulus, shear_modulus, density = fields
        inverse_volume = 1.0 / volume
        shear[i + HORIZON, inner_y] = 15.0 * shear_modulus * inverse_volume
        pressure_ratio = (3.0 * bulk_modulus - 5.0 * shear_modulus) * inverse_volume
        ratio[i] = 3.0 * pressure_ratio * inverse_volume
        inverse_mass[i] = 1.0 / density

    every(weigh)
    fetch_disp.wait()
    neighbours = (
        1 + (gx > 0).astype(jnp.int32) + (gx < size_x - 1).astype(jnp.int32)
    ) * (1 + (gy > 0).astype(jnp.int32) + (gy < size_y - 1).astype(jnp.int32)) - 1
    pl.semaphore_wait(barrier, neighbours)

    send(disp, (slice(None),), 0)
    send(shear, (), 1)

    def stretch(i, pairs, total):
        centre = [disp[k, i + HORIZON, inner_y] for k in range(3)]
        for a, b in pairs:
            rows = pl.ds(ROW_PAD + b, block_y)
            near = [disp[k, i + HORIZON + a, rows] for k in range(3)]
            flat_near, flat_here = None, None
            for k, factor in ((0, a), (1, b)):
                flat_near = plus(flat_near, near[k], factor)
                flat_here = plus(flat_here, centre[k], factor)
            for c, number, radius in column(a, b):
                along = ahead(plus(flat_near, near[2], c), c) - plus(flat_here, centre[2], c)
                part = weight[number, i] * along
                total = plus(total, part)
                term[number, i] = part if radius == 1 else part * (1.0 / radius)
        return total

    def stretch_level(i):
        partial[i] = stretch(i, LEVEL, None)

    def stretch_rest(i):
        pressure[i + HORIZON, inner_y] = stretch(i, SLANTED, partial[i]) * ratio[i]

    def turn(i):
        for a, b in SLANTED:
            for c, number, radius in column(a, b):
                if c != 0:
                    turned[number, i] = ahead(weight[number, i], -c)

    every(turn)
    receive(disp, (slice(None),), 0, X_FACES)
    every(stretch_level)
    receive(disp, (slice(None),), 0, Y_FACES)
    inner(stretch_rest)
    receive(disp, (slice(None),), 0, CORNERS)
    outer(stretch_rest)
    send(pressure, (), 2)
    receive(shear, (), 1, X_FACES + Y_FACES + CORNERS)

    def pull(i):
        shear_here = shear[i + HORIZON, inner_y]
        pressure_here = pressure[i + HORIZON, inner_y]
        force = [None, None, None]
        for a, b in PAIRS:
            near = shear[i + HORIZON + a, pl.ds(ROW_PAD + b, block_y)]
            level = None
            for c, number, radius in column(a, b):
                part = weight[number, i] * pressure_here
                part = part + term[number, i] * (ahead(near, c) + shear_here)
                level = plus(level, part)
                force[2] = plus(force[2], part, c)
            force[0] = plus(force[0], level, a)
            force[1] = plus(force[1], level, b)
        for k in range(3):
            accel[k, i] = force[k]

    def push_level(i):
        force = [accel[k, i] for k in range(3)]
        for a, b in LEVEL:
            near = pressure[i + HORIZON + a, inner_y]
            level = None
            for c, number, radius in column(a, b):
                part = weight[number, i] * ahead(near, c)
                level = plus(level, part)
                force[2] = plus(force[2], part, c)
            force[0] = plus(force[0], level, a)
        for k in range(3):
            accel[k, i] = force[k]

    def push_slanted(i):
        force = [accel[k, i] for k in range(3)]
        for c in range(-HORIZON, HORIZON + 1):
            source = weight if c == 0 else turned
            sums = [None, None, None]
            for a in range(-HORIZON, HORIZON + 1):
                row = None
                for b in range(1, HORIZON + 1):
                    if (a, b, c) in NUMBER:
                        up, down = (
                            source[NUMBER[(a, side, c)], i]
                            * pressure[i + HORIZON + a, pl.ds(ROW_PAD + side, block_y)]
                            for side in (b, -b)
                        )
                        row = plus(row, up + down)
                        sums[1] = plus(sums[1], up - down, b)
                if row is not None:
                    sums[0] = plus(sums[0], row, a)
                    sums[2] = plus(sums[2], row)
            if sums[2] is not None:
                for k, factor in ((0, 1), (1, 1), (2, c)):
                    if factor != 0:
                        force[k] = plus(force[k], ahead(sums[k], c), factor)
        for k in range(3):
            accel[k, i] = force[k] * inverse_mass[i]

    every(pull)
    receive(pressure, (), 2, X_FACES)
    every(push_level)
    receive(pressure, (), 2, Y_FACES)
    inner(push_slanted)
    receive(pressure, (), 2, CORNERS)
    outer(push_slanted)
    sent(disp, (slice(None),), 0)
    sent(shear, (), 1)
    sent(pressure, (), 2)


def on_device(displacement, velocity, region, bond_words, moduli):
    block = region.shape
    padded = (block[0] + 2 * HORIZON, block[1] + 2 * ROW_PAD, block[2])
    anywhere = pl.BlockSpec(memory_space=pl.ANY)
    bonds = len(OFFSETS)
    places = len(DIRECTIONS)
    acceleration = pl.pallas_call(
        kernel,
        out_shape=pltpu.VMEM(displacement.shape, jnp.float32),
        in_specs=[anywhere] * 4,
        out_specs=pl.BlockSpec(memory_space=pltpu.VMEM),
        scratch_shapes=[
            pltpu.VMEM((3,) + padded, jnp.float32),
            pltpu.VMEM(padded, jnp.float32),
            pltpu.VMEM(padded, jnp.float32),
            pltpu.VMEM(block, jnp.int32),
            pltpu.VMEM(bond_words.shape, jnp.int32),
            pltpu.VMEM((bonds,) + block, jnp.float32),
            pltpu.VMEM((bonds,) + block, jnp.float32),
            pltpu.VMEM(block, jnp.float32),
            pltpu.VMEM(block, jnp.float32),
            pltpu.VMEM(block, jnp.float32),
            pltpu.VMEM((bonds,) + block, jnp.float32),
            pltpu.SMEM(moduli.shape, jnp.float32),
            pltpu.SemaphoreType.DMA((4,)),
            pltpu.SemaphoreType.DMA((3, places)),
            pltpu.SemaphoreType.DMA((3, places)),
        ],
        compiler_params=pltpu.CompilerParams(collective_id=0, has_side_effects=True),
        name="peridynamic",
    )(displacement, region, bond_words, moduli)
    new_velocity = velocity + time_step * acceleration
    return (displacement + time_step * new_velocity, new_velocity)


def solution(mesh):
    placed = (
        P(None, "gx", "gy", None),
        P(None, "gx", "gy", None),
        P("gx", "gy", None),
        P(None, "gx", "gy", None),
        P(),
    )
    return jax.shard_map(
        on_device,
        mesh=mesh,
        in_specs=placed,
        out_specs=(P(None, "gx", "gy", None), P(None, "gx", "gy", None)),
        check_vma=False,
    )
```
